256 devices in a mesh: row: 16 (over z, x_lo), col: 16 (over x_hi, y, core).
Axes of the slice: x: 4 (x_hi: 2, x_lo: 2; x = x_hi * 2 + x_lo), y: 4, z: 8, core: 2. Of those that a mesh axis runs over, the one named last changes fastest.
Arguments:
- hidden: bfloat16 [196608, 6144], P(('row', 'col')), may hold values from -700 to 700
- gain: float32 [6144], replicated, may hold values from 0.5 to 1.5
- d_query: bfloat16 [196608, 512], P(('row', 'col')), may hold values from -0.03125 to 0.03125
Outputs:
- weight_grad: float32 [6144, 512], P('row')
The draws below stay inside these ranges and needn't reach their ends.
All inputs are finite; a program needn't handle non-finite values.
Results may differ from the reference program's by a relative error of at most 0.0029.
Values sent between devices are 32-bit elements; how exact they have to be, the bound alone decides.
A program may use at most 64 MiB of HBM per device.

```python
import jax
import jax.numpy as jnp
from jax import lax

D = 6144
C = 512
TOKENS = 196608


def draw_hidden(key, part):
    keys = jax.random.split(jax.random.fold_in(key, 17), 3)
    token_scale = jnp.exp(jax.random.uniform(keys[0], (TOKENS, 1), jnp.float32, 0.0, jnp.log(10.0)))
    feature_scale = jnp.exp(jax.random.uniform(keys[1], (1, D), jnp.float32, 0.0, jnp.log(10.0)))
    noise = jnp.clip(jax.random.normal(keys[2], (TOKENS, D), jnp.float32), -6.0, 6.0)
    values = noise * token_scale * feature_scale
    return jnp.clip(values, -700.0, 700.0).astype(jnp.bfloat16)


def shard_levels(own_key, dims, cuts, least, largest):
    factor_of, own = 1.0, jax.random.fold_in(own_key, 6)
    for dim, parts in cuts:
        draws = jnp.exp(jax.random.uniform(jax.random.fold_in(own, dim), (parts,), jnp.float32, least / len(cuts), largest / len(cuts)))
        factor_of = factor_of * jnp.repeat(draws, dims[dim] // parts).reshape([-1 if axis == dim else 1 for axis in range(len(dims))])
    return factor_of


def gaussian(own_key, dims, deviation, limit, cuts=(), kind=jnp.bfloat16):
    array = jax.random.normal(own_key, dims, jnp.float32) * deviation
    if len(cuts) > 0:
        array = shard_levels(own_key, dims, cuts, -0.22, 0.18) * array
    return jnp.clip(array, min=-limit, max=limit).astype(kind)


def setup_inputs(seed: int = 0) -> dict:
    seeds = jax.random.split(jax.random.key(seed), 4)
    hidden = draw_hidden(jax.random.fold_in(seeds[3], 71), 0)
    gain = jnp.clip(1.0 + 0.1 * jax.random.normal(seeds[1], (D,), jnp.float32), 0.5, 1.5)
    d_query = gaussian(seeds[2], (TOKENS, C), (TOKENS ** -0.5), 0.03125, ((0, 256),))
    return {"hidden": hidden, "gain": gain, "d_query": d_query}


def reference(hidden, gain, d_query):
    block_rows = 4096 if TOKENS % 4096 == 0 else TOKENS
    count = TOKENS // block_rows

    def accumulate(total, index):
        start = (index * block_rows).astype(jnp.int32)
        values = lax.dynamic_slice_in_dim(hidden, start, block_rows, 0).astype(jnp.float32)
        average = lax.optimization_barrier(jnp.mean(values, axis=1, keepdims=True))
        centred = values - average
        spread = lax.optimization_barrier(jnp.mean(centred * centred, axis=1, keepdims=True))
        normed = (centred * lax.rsqrt(spread + 1e-06) * gain.astype(jnp.float32)).astype(jnp.bfloat16)
        cotangent = lax.dynamic_slice_in_dim(d_query, start, block_rows, 0)
        product = lax.dot_general(normed, cotangent, (((0,), (0,)), ((), ())), preferred_element_type=jnp.float32)
        return (total + product, None)
    start_total = jnp.zeros((D, C), jnp.float32)
    total, unused = lax.scan(accumulate, start_total, jnp.arange(count, dtype=jnp.int32))
    return total
```

```python
import jax
import jax.numpy as jnp
from jax import lax
from jax.experimental import pallas as pl
from jax.experimental.pallas import tpu as pltpu
from jax.sharding import PartitionSpec as P

D = 6144
C = 512
T = 768
ROWS = 384
HALF = C // 2
SA, SB, SC = 4, 4, 4
A0, B0, C0 = 0, 8 * SA, 8 * (SA + SB)
NA, NB, NC = 8 * SA, 8 * SB, 8 * SC
ORDER = (4, 3, -3, 2, -2, 1, -1, 0)
SUB = 64
F32 = jnp.float32
MESH = pl.DeviceIdType.MESH
N_SEM = 160


def kernel(
    h_hbm, gain, dq_hbm, out_hbm,
    h, dq_own, dq_peer, nb, mean_s, rstd_s, S, X, RP, RA, RB, RC, TB, TC, TA, RB2, RC2, U, RZ, RA2, PF, O,
    in_sem, out_sem, ss, rs,
):
    r, c = lax.axis_index("row"), lax.axis_index("col")
    z, xlo = r // 2, lax.rem(r, 2)
    xhi, y, core = c // 8, lax.rem(c // 2, 4), lax.rem(c, 2)
    x = xhi * 2 + xlo

    def device(dx=0, dy=0, dz=0, flip=0):
        nx, ny = lax.rem(x + dx + 4, 4), lax.rem(y + dy + 4, 4)
        nz, ncore = lax.rem(z + dz + 8, 8), lax.rem(core + flip, 2)
        return (nz * 2 + lax.rem(nx, 2), (nx // 2) * 8 + ny * 2 + ncore)

    def lanes(block, width=128):
        return pl.ds(pl.multiple_of(block * width, width), width)

    count = [0]
    sent = []

    def send(src, dst, **where):
        k = count[0]
        count[0] += 1
        copy = pltpu.make_async_remote_copy(
            src, dst, ss.at[k], rs.at[k], device_id=device(**where), device_id_type=MESH
        )
        copy.start()
        sent.append(copy)
        return copy

    loads = [
        pltpu.make_async_copy(h_hbm.at[pl.ds(k * 128, 128)], h.at[pl.ds(k * 128, 128)], in_sem.at[k])
        for k in range(T // 128)
    ]
    for copy in loads:
        copy.start()
    load_own = pltpu.make_async_copy(dq_hbm.at[:, lanes(core, HALF)], dq_own, in_sem.at[6])
    load_peer = pltpu.make_async_copy(dq_hbm.at[:, lanes(1 - core, HALF)], dq_peer, in_sem.at[7])
    load_own.start()
    load_peer.start()

    plane = [(dx, dy) for dx in range(4) for dy in range(4) if (dx, dy) != (0, 0)]
    barrier = pltpu.get_barrier_semaphore()
    partners = [dict(flip=1)] + [dict(dz=k) for k in range(1, 8)] + [dict(dx=dx, dy=dy) for dx, dy in plane]
    for where in partners:
        pl.semaphore_signal(barrier, inc=1, device_id=device(**where), device_id_type=MESH)

    for k, copy in enumerate(loads):
        copy.wait()

        @pl.loop(0, 128 // SUB)
        def _(b):
            rows = pl.ds(pl.multiple_of(k * 128 + b * SUB, SUB), SUB)
            total = jnp.zeros((SUB, 128), F32)
            for t in range(D // 128):
                total += h[rows, t * 128 : (t + 1) * 128].astype(F32)
            mean = jnp.broadcast_to(jnp.sum(total, axis=1, keepdims=True) * (1.0 / D), (SUB, 128))
            square = jnp.zeros((SUB, 128), F32)
            for t in range(D // 128):
                centred = h[rows, t * 128 : (t + 1) * 128].astype(F32) - mean
                square += centred * centred
            var = jnp.broadcast_to(jnp.sum(square, axis=1, keepdims=True) * (1.0 / D), (SUB, 128))
            mean_s[rows, :] = mean
            rstd_s[rows, :] = lax.rsqrt(var + 1e-06)

    load_own.wait()
    load_peer.wait()
    pl.semaphore_wait(barrier, len(partners))

    def work(i, dz):
        base = lax.rem(z + dz + 8, 8) * (2 * ROWS)

        @pl.loop(0, T // SUB)
        def _(b):
            rows = pl.ds(pl.multiple_of(b * SUB, SUB), SUB)
            mean, rstd = mean_s[rows, :], rstd_s[rows, :]
            for t in range(2 * ROWS // 128):
                cols = pl.ds(pl.multiple_of(base + t * 128, 128), 128)
                centred = h[rows, cols].astype(F32) - mean
                nb[rows, t * 128 : (t + 1) * 128] = (centred * rstd * gain[:, cols]).astype(jnp.bfloat16)

        for g in range(2):
            left = nb[:, g * ROWS : (g + 1) * ROWS]
            for out, right in ((X, dq_peer), (S, dq_own)):
                out[i, g] = lax.dot_general(
                    left, right[...], (((0,), (0,)), ((), ())), preferred_element_type=F32
                ).reshape(4, ROWS // 4, HALF)

    def pair_add(i):
        @pl.loop(0, 8)
        def _(k):
            S[i, k // 4, lax.rem(k, 4)] += RP[i, k // 4, lax.rem(k, 4)]

    def target_x(dx):
        nx = lax.rem(x + dx + 4, 4)
        return lax.rem(nx, 2), nx // 2

    def target_y(dy):
        return lax.rem(y + dy + 4, 4)

    def b_block(i, n, dx, half):
        low, high = target_x(dx)
        return (pl.ds(i, n), low, pl.ds(half * 2, 2), pl.ds(B0, NB), lanes(high))

    def c_block(i, n, dy, half):
        return (pl.ds(i, n), half, target_y(dy), pl.ds(C0, NC))

    def a_block(i, g):
        return (i, g, slice(None), pl.ds(A0, NA))

    ring = {}

    def ring_first(j):
        i = 2 * j
        for s, (R, block, axis) in enumerate(((RB, b_block, "dx"), (RC, c_block, "dy"))):
            ring[s, j] = [
                send(S.at[block(i, 2, 2, 0)], R.at[j, 0], **{axis: 1}),
                send(S.at[block(i, 2, 2, 1)], R.at[j, 1], **{axis: -1}),
                send(S.at[block(i, 2, 1, 1)], R.at[j, 2], **{axis: 1}),
                send(S.at[block(i, 2, -1, 0)], R.at[j, 3], **{axis: -1}),
            ]

    def ring_second(j):
        i = 2 * j
        for s, (R, block, axis) in enumerate(((RB, b_block, "dx"), (RC, c_block, "dy"))):
            for slot, d, half in ((0, 1, 0), (1, -1, 1)):
                ring[s, j][slot].wait_recv()
                R[j, slot] += S[block(i, 2, d, half)]
                ring[s, j].append(send(R.at[j, slot], R.at[j, 4 + slot], **{axis: d}))

    def ring_end(j):
        i = 2 * j
        for s in range(2):
            for slot in range(2, 6):
                ring[s, j][slot].wait_recv()
        for half, (p, q) in enumerate(((3, 4), (2, 5))):
            TB[pl.ds(i, 2), pl.ds(half * 2, 2)] = S[b_block(i, 2, 0, half)] + RB[j, p] + RB[j, q]
            TC[pl.ds(i, 2), half] = S[c_block(i, 2, 0, half)] + RC[j, p] + RC[j, q]

    up = ((0, 0, 0, None), (1, 1, 1, None), (2, 1, 0, 0), (3, 3, 1, 1), (4, 3, 0, 2), (5, 5, 1, 3), (6, 5, 0, 4))
    down = ((7, 0, 1, None), (8, 2, 0, None), (9, 2, 1, 7), (10, 4, 0, 8), (11, 4, 1, 9), (12, 6, 0, 10), (13, 6, 1, 11))
    a_sent = {}

    def a_step(k):
        for (slot, i, g, add), dz in ((up[k], 1), (down[k], -1)):
            if add is None:
                a_sent[slot] = send(S.at[a_block(i, g)], RA.at[slot], dz=dz)
            else:
                a_sent[add].wait_recv()
                RA[add] += S[a_block(i, g)]
                a_sent[slot] = send(RA.at[add], RA.at[slot], dz=dz)

    pairs = {}

    def start_pair(i):
        pairs[i] = send(X.at[i], RP.at[i], flip=1)

    def finish_pair(i):
        pairs[i].wait_recv()
        pair_add(i)

    for i, dz in enumerate(ORDER):
        work(i, dz)
        start_pair(i)
        if i >= 1:
            finish_pair(i - 1)
            if i == 1:
                a_step(0)
            if i == 3:
                a_step(1)
            if i % 2 == 0:
                ring_first(i // 2 - 1)
        if i == 5:
            a_step(2)
        if i in (4, 6):
            ring_second(i // 2 - 2)
    finish_pair(7)
    ring_first(3)

    second = {}

    def stage2(q):
        i = 4 * q
        for k in range(1, 4):
            low, high = target_x(k)
            second[0, q, k] = send(TB.at[pl.ds(i, 4), target_y(k)], RB2.at[q, k - 1], dy=k)
            second[1, q, k] = send(TC.at[pl.ds(i, 4), low, :, lanes(high)], RC2.at[q, k - 1], dx=k)

    third = {}

    def stage3(q):
        i = 4 * q
        for k in range(1, 4):
            second[0, q, k].wait_recv()
            second[1, q, k].wait_recv()
        part_b = TB[pl.ds(i, 4), y]
        part_c = TC[pl.ds(i, 4), xlo, :, lanes(xhi)]
        for k in range(3):
            part_b += RB2[q, k]
            part_c += RC2[q, k]
        U[pl.ds(i, 4), 0:NB] = part_b
        U[pl.ds(i, 4), NB : NB + NC] = part_c
        for k in range(i, min(i + 4, 7)):
            third[k] = send(U.at[k], RZ.at[k], dz=ORDER[k])

    a_step(3)
    ring_second(2)
    ring_end(0)
    a_step(4)
    ring_second(3)
    ring_end(1)
    stage2(0)
    a_step(5)
    ring_end(2)
    a_step(6)
    ring_end(3)
    stage2(1)
    stage3(0)
    stage3(1)

    for g, (p, q) in enumerate(((6, 12), (5, 13))):
        a_sent[p].wait_recv()
        a_sent[q].wait_recv()
        TA[g] = S[a_block(7, g)] + RA[p] + RA[q]
    a_plane = []
    for k, (dx, dy) in enumerate(plane):
        low, high = target_x(dx)
        a_plane.append(send(TA.at[low, target_y(dy), :, lanes(high)], RA2.at[k], dx=dx, dy=dy))

    mine = lanes(core * 2 + xhi)
    owners = [(dx, dy) for dx, dy in plane if dx in (0, 2)]
    gathered = []

    def gather(first, n):
        O[y, pl.ds(first, n), mine] = PF[pl.ds(first, n)]
        for dx, dy in owners:
            gathered.append(send(PF.at[pl.ds(first, n)], O.at[y, pl.ds(first, n), mine], dx=dx, dy=dy))

    for k in range(7):
        third[k].wait_recv()
    total = U[7]
    for k in range(7):
        total += RZ[k]
    PF[B0 : B0 + NB + NC] = total
    gather(B0, NB + NC)

    total = TA[xlo, y, :, lanes(xhi)]
    for k in range(15):
        a_plane[k].wait_recv()
        total += RA2[k]
    PF[A0 : A0 + NA] = total
    gather(A0, NA)

    for copy in gathered:
        copy.wait_recv()
    half = lanes(core, HALF)
    other = lanes(1 - core, HALF)
    forward = send(O.at[:, :, half], O.at[:, :, half], flip=1)
    store = pltpu.make_async_copy(O.at[:, :, half], out_hbm.at[:, :, half], out_sem.at[0])
    store.start()
    forward.wait_recv()
    store_other = pltpu.make_async_copy(O.at[:, :, other], out_hbm.at[:, :, other], out_sem.at[1])
    store_other.start()
    for copy in sent:
        copy.wait_send()
    store.wait()
    store_other.wait()


def per_device(hidden, gain, d_query):
    q = ROWS // 4
    scratch = [
        pltpu.VMEM((T, D), jnp.bfloat16),
        pltpu.VMEM((T, HALF), jnp.bfloat16),
        pltpu.VMEM((T, HALF), jnp.bfloat16),
        pltpu.VMEM((T, 2 * ROWS), jnp.bfloat16),
        pltpu.VMEM((T, 128), F32),
        pltpu.VMEM((T, 128), F32),
        pltpu.VMEM((8, 2, 4, q, HALF), F32),
        pltpu.VMEM((8, 2, 4, q, HALF), F32),
        pltpu.VMEM((8, 2, 4, q, HALF), F32),
        pltpu.VMEM((14, 4, NA, HALF), F32),
        pltpu.VMEM((4, 6, 2, 2, NB, 128), F32),
        pltpu.VMEM((4, 6, 2, NC, HALF), F32),
        pltpu.VMEM((8, 4, NB, 128), F32),
        pltpu.VMEM((8, 2, NC, HALF), F32),
        pltpu.VMEM((2, 4, NA, HALF), F32),
        pltpu.VMEM((2, 3, 4, NB, 128), F32),
        pltpu.VMEM((2, 3, 4, NC, 128), F32),
        pltpu.VMEM((8, NB + NC, 128), F32),
        pltpu.VMEM((7, NB + NC, 128), F32),
        pltpu.VMEM((15, NA, 128), F32),
        pltpu.VMEM((q, 128), F32),
        pltpu.VMEM((4, q, C), F32),
        pltpu.SemaphoreType.DMA((8,)),
        pltpu.SemaphoreType.DMA((2,)),
        pltpu.SemaphoreType.DMA((N_SEM,)),
        pltpu.SemaphoreType.DMA((N_SEM,)),
    ]
    out = pl.pallas_call(
        kernel,
        out_shape=jax.ShapeDtypeStruct((4, q, C), F32),
        in_specs=[
            pl.BlockSpec(memory_space=pl.ANY),
            pl.BlockSpec(memory_space=pltpu.VMEM),
            pl.BlockSpec(memory_space=pl.ANY),
        ],
        out_specs=pl.BlockSpec(memory_space=pl.ANY),
        scratch_shapes=scratch,
        compiler_params=pltpu.CompilerParams(
            collective_id=0, has_side_effects=True, vmem_limit_bytes=58 << 20
        ),
    )(hidden, gain.reshape(1, D), d_query)
    return out.reshape(ROWS, C)


def solution(mesh):
    both = ("row", "col")
    return jax.shard_map(
        per_device,
        mesh=mesh,
        in_specs=(P(both, None), P(), P(both, None)),
        out_specs=P("row", None),
        check_vma=False,
    )
```

```python
import jax
import jax.numpy as jnp
from jax import lax
from jax.experimental import pallas as pl
from jax.experimental.pallas import tpu as pltpu
from jax.sharding import PartitionSpec as P

D = 6144
C = 512
T = 768
ROWS = 384
HALF = C // 2
CHUNKS = ((3, 4, 4, 4),)
ORDER = (4, 3, -3, 2, -2, 1, -1, 0)
WORK, FIN, A_STEP, RING_FIRST, RING_SECOND, RING_END, STAGE3, A_END, BC_END, A_GATHER, FORWARD, FINISH = range(12)
EVENTS = (
    (WORK, 0, 0), (WORK, 0, 1), (WORK, 0, 2), (FIN, 0, 0), (A_STEP, 0, 0), (WORK, 0, 3),
    (FIN, 0, 1), (RING_FIRST, 0, 0), (WORK, 0, 4), (FIN, 0, 2), (A_STEP, 0, 1), (WORK, 0, 5),
    (FIN, 0, 3), (RING_FIRST, 0, 1), (A_STEP, 0, 2), (WORK, 0, 6), (FIN, 0, 4), (RING_SECOND, 0, 0),
    (WORK, 0, 7), (FIN, 0, 5), (RING_FIRST, 0, 2), (A_STEP, 0, 3), (FIN, 0, 6), (FIN, 0, 7),
    (RING_FIRST, 0, 3), (RING_SECOND, 0, 1), (A_STEP, 0, 4), (RING_END, 0, 0), (RING_SECOND, 0, 2), (A_STEP, 0, 5),
    (RING_END, 0, 1), (RING_SECOND, 0, 3), (STAGE3, 0, 0), (A_STEP, 0, 6), (RING_END, 0, 2), (STAGE3, 0, 1),
    (RING_END, 0, 3), (STAGE3, 0, 2), (A_END, 0, 0), (STAGE3, 0, 3), (BC_END, 0, 0), (A_GATHER, 0, 0),
    (FORWARD, 0, 0), (FINISH, 0, 0),
)
SUB = 32
WSUB = 64
F32 = jnp.float32
MESH = pl.DeviceIdType.MESH
N_SEM = 144 * len(CHUNKS)


def kernel(h_hbm, gain, dq_hbm, O, h, dq_own, dq_peer, nb, mean_s, rstd_s, in_sem, ss, rs, *buffers):
    r, c = lax.axis_index("row"), lax.axis_index("col")
    z, xlo = r // 2, lax.rem(r, 2)
    xhi, y, core = c // 8, lax.rem(c // 2, 4), lax.rem(c, 2)
    x = xhi * 2 + xlo

    def device(dx=0, dy=0, dz=0, flip=0):
        nx, ny = lax.rem(x + dx + 4, 4), lax.rem(y + dy + 4, 4)
        nz, ncore = lax.rem(z + dz + 8, 8), lax.rem(core + flip, 2)
        return (nz * 2 + lax.rem(nx, 2), (nx // 2) * 8 + ny * 2 + ncore)

    def lanes(block, width=128):
        return pl.ds(pl.multiple_of(block * width, width), width)

    count = [0]
    sent = []

    def send(src, dst, **where):
        k = count[0]
        count[0] += 1
        copy = pltpu.make_async_remote_copy(
            src, dst, ss.at[k], rs.at[k], device_id=device(**where), device_id_type=MESH
        )
        copy.start()
        sent.append(copy)
        return copy

    loads = [
        pltpu.make_async_copy(h_hbm.at[pl.ds(k * 128, 128)], h.at[pl.ds(k * 128, 128)], in_sem.at[k])
        for k in range(T // 128)
    ]
    for copy in loads:
        copy.start()
    load_own = pltpu.make_async_copy(dq_hbm.at[:, lanes(core, HALF)], dq_own, in_sem.at[6])
    load_peer = pltpu.make_async_copy(dq_hbm.at[:, lanes(1 - core, HALF)], dq_peer, in_sem.at[7])
    load_own.start()
    load_peer.start()

    plane = [(dx, dy) for dx in range(4) for dy in range(4) if (dx, dy) != (0, 0)]
    barrier = pltpu.get_barrier_semaphore()
    partners = [dict(flip=1)] + [dict(dz=k) for k in range(1, 8)] + [dict(dx=dx, dy=dy) for dx, dy in plane]
    for where in partners:
        pl.semaphore_signal(barrier, inc=1, device_id=device(**where), device_id_type=MESH)

    for k, copy in enumerate(loads):
        copy.wait()

        @pl.loop(0, 128 // SUB, unroll=True)
        def _(b):
            rows = pl.ds(pl.multiple_of(k * 128 + b * SUB, SUB), SUB)
            first = h[rows, 0:128].astype(F32)
            shift = jnp.broadcast_to(jnp.sum(first, axis=1, keepdims=True) * (1.0 / 128), (SUB, 128))
            total = jnp.zeros((SUB, 128), F32)
            square = jnp.zeros((SUB, 128), F32)
            for t in range(D // 128):
                apart = h[rows, t * 128 : (t + 1) * 128].astype(F32) - shift
                total += apart
                square += apart * apart
            off = jnp.sum(total, axis=1, keepdims=True) * (1.0 / D)
            var = jnp.maximum(jnp.sum(square, axis=1, keepdims=True) * (1.0 / D) - off * off, 0.0)
            mean_s[rows, :] = shift + jnp.broadcast_to(off, (SUB, 128))
            rstd_s[rows, :] = jnp.broadcast_to(lax.rsqrt(var + 1e-06), (SUB, 128))

    load_own.wait()
    load_peer.wait()
    pl.semaphore_wait(barrier, len(partners))

    def target_x(dx):
        nx = lax.rem(x + dx + 4, 4)
        return lax.rem(nx, 2), nx // 2

    def target_y(dy):
        return lax.rem(y + dy + 4, 4)

    mine = lanes(core * 2 + xhi)
    half_mine = lanes(core, HALF)
    owners = [(dx, dy) for dx, dy in plane if dx in (0, 2)]

    def chunk(q):
        w, na, nb_, nc = (v * m for v, m in zip(CHUNKS[q], (1, 8, 8, 8)))
        tile0 = sum(CHUNKS[k][0] for k in range(q))
        b0, c0 = na, na + nb_
        per_y = 32 * w
        S, X, RP, RA, RB, RC, TB, TC, TA, RB2, RC2, U, RZ, RA2, PF = buffers[q * 15 : q * 15 + 15]
        pairs, ring, second, third, a_sent, a_plane, gathered, last = {}, {}, {}, {}, {}, [], [], []

        def normalise(i, slot):
            group = lax.rem(z + ORDER[i] + 8, 8) * 2
            for b in range(T // WSUB):
                rows = pl.ds(b * WSUB, WSUB)
                mean, rstd = mean_s[rows, :], rstd_s[rows, :]
                for t in range(2 * w):
                    cols = lanes((group + t // w) * 3 + tile0 + t % w)
                    centred = h[rows, cols].astype(F32) - mean
                    nb[slot, rows, t * 128 : (t + 1) * 128] = (centred * rstd * gain[:, cols]).astype(jnp.bfloat16)

        def work(i):
            slot = i % 2

            def product(out, right):
                out[i] = lax.dot_general(
                    nb[slot, :, : 256 * w], right[...], (((0,), (0,)), ((), ())), preferred_element_type=F32
                ).reshape(2, 4, per_y, HALF)

            product(X, dq_peer)
            pairs[i] = send(X.at[i], RP.at[i], flip=1)
            product(S, dq_own)
            if i < 7:
                normalise(i + 1, 1 - slot)
            elif q + 1 < len(CHUNKS):
                chunks[q + 1][-1](0, 1 - slot)

        def fin(i):
            pairs[i].wait_recv()
            S[i] += RP[i]

        def b_block(i, dx, half):
            low, high = target_x(dx)
            return (pl.ds(i, 2), low, pl.ds(half * 2, 2), pl.ds(b0, nb_), lanes(high))

        def c_block(i, dy, half):
            return (pl.ds(i, 2), half, target_y(dy), pl.ds(c0, nc))

        def a_block(i, g):
            return (i, g, slice(None), pl.ds(0, na))

        both = ((RB, b_block, "dx"), (RC, c_block, "dy"))

        def ring_first(j):
            i = 2 * j
            for s, (R, block, axis) in enumerate(both):
                ring[s, j] = [
                    send(S.at[block(i, 2, 0)], R.at[j, 0], **{axis: 1}),
                    send(S.at[block(i, 2, 1)], R.at[j, 1], **{axis: -1}),
                    send(S.at[block(i, 1, 1)], R.at[j, 2], **{axis: 1}),
                    send(S.at[block(i, -1, 0)], R.at[j, 3], **{axis: -1}),
                ]

        def ring_second(j):
            i = 2 * j
            for s, (R, block, axis) in enumerate(both):
                for slot, d, half in ((0, 1, 0), (1, -1, 1)):
                    ring[s, j][slot].wait_recv()
                    R[j, slot] += S[block(i, d, half)]
                    ring[s, j].append(send(R.at[j, slot], R.at[j, 4 + slot], **{axis: d}))

        def ring_end(j):
            i = 2 * j
            for s in range(2):
                for slot in range(2, 6):
                    ring[s, j][slot].wait_recv()
            for half, (p, r) in enumerate(((3, 4), (2, 5))):
                TB[pl.ds(i, 2), pl.ds(half * 2, 2)] = S[b_block(i, 0, half)] + RB[j, p] + RB[j, r]
                TC[pl.ds(i, 2), half] = S[c_block(i, 0, half)] + RC[j, p] + RC[j, r]
            for k in range(1, 4):
                low, high = target_x(k)
                second[0, j, k] = send(TB.at[pl.ds(i, 2), target_y(k)], RB2.at[j, k - 1], dy=k)
                second[1, j, k] = send(TC.at[pl.ds(i, 2), low, :, lanes(high)], RC2.at[j, k - 1], dx=k)

        def stage3(j):
            i = 2 * j
            for k in range(1, 4):
                second[0, j, k].wait_recv()
                second[1, j, k].wait_recv()
            part_b = TB[pl.ds(i, 2), y]
            part_c = TC[pl.ds(i, 2), xlo, :, lanes(xhi)]
            for k in range(3):
                part_b += RB2[j, k]
                part_c += RC2[j, k]
            U[pl.ds(i, 2), 0:nb_] = part_b
            U[pl.ds(i, 2), nb_ : nb_ + nc] = part_c
            for k in range(i, min(i + 2, 7)):
                third[k] = send(U.at[k], RZ.at[k], dz=ORDER[k])

        up = ((0, 0, 0, None), (1, 1, 1, None), (2, 1, 0, 0), (3, 3, 1, 1), (4, 3, 0, 2), (5, 5, 1, 3), (6, 5, 0, 4))
        down = ((7, 0, 1, None), (8, 2, 0, None), (9, 2, 1, 7), (10, 4, 0, 8), (11, 4, 1, 9), (12, 6, 0, 10), (13, 6, 1, 11))

        def a_step(k):
            for (slot, i, g, add), dz in ((up[k], 1), (down[k], -1)):
                if add is None:
                    a_sent[slot] = send(S.at[a_block(i, g)], RA.at[slot], dz=dz)
                else:
                    a_sent[add].wait_recv()
                    RA[add] += S[a_block(i, g)]
                    a_sent[slot] = send(RA.at[add], RA.at[slot], dz=dz)

        def a_end(_):
            for g, (p, r) in enumerate(((6, 12), (5, 13))):
                a_sent[p].wait_recv()
                a_sent[r].wait_recv()
                TA[g] = S[a_block(7, g)] + RA[p] + RA[r]
            for k, (dx, dy) in enumerate(plane):
                low, high = target_x(dx)
                a_plane.append(send(TA.at[low, target_y(dy), :, lanes(high)], RA2.at[k], dx=dx, dy=dy))

        def gather(first, n):
            rows = pl.ds(pl.multiple_of(tile0 * 128 + y * per_y + first, 8), n)
            O[rows, mine] = PF[pl.ds(first, n)]
            for dx, dy in owners:
                gathered.append(send(PF.at[pl.ds(first, n)], O.at[rows, mine], dx=dx, dy=dy))

        def bc_end(_):
            for k in range(7):
                third[k].wait_recv()
            total = U[7]
            for k in range(7):
                total += RZ[k]
            PF[b0:per_y] = total
            gather(b0, nb_ + nc)

        def a_gather(_):
            total = TA[xlo, y, :, lanes(xhi)]
            for k in range(15):
                a_plane[k].wait_recv()
                total += RA2[k]
            PF[0:na] = total
            gather(0, na)

        def forward(_):
            for copy in gathered:
                copy.wait_recv()
            part = O.at[pl.ds(tile0 * 128, 128 * w), half_mine]
            last.append(send(part, part, flip=1))

        def finish(_):
            last[0].wait_recv()

        return (work, fin, a_step, ring_first, ring_second, ring_end, stage3, a_end, bc_end, a_gather, forward, finish, normalise)

    chunks = [chunk(q) for q in range(len(CHUNKS))]
    chunks[0][-1](0, 0)
    for event, q, k in EVENTS:
        chunks[q][event](k)
    for copy in sent:
        copy.wait_send()


def per_device(hidden, gain, d_query):
    scratch = [
        pltpu.VMEM((T, D), jnp.bfloat16),
        pltpu.VMEM((T, HALF), jnp.bfloat16),
        pltpu.VMEM((T, HALF), jnp.bfloat16),
        pltpu.VMEM((2, T, 256 * max(w for w, *_ in CHUNKS)), jnp.bfloat16),
        pltpu.VMEM((T, 128), F32),
        pltpu.VMEM((T, 128), F32),
        pltpu.SemaphoreType.DMA((8,)),
        pltpu.SemaphoreType.DMA((N_SEM,)),
        pltpu.SemaphoreType.DMA((N_SEM,)),
    ]
    for w, a, b, c in CHUNKS:
        na, nb, nc, per_y = 8 * a, 8 * b, 8 * c, 32 * w
        scratch += [
            pltpu.VMEM(shape, F32)
            for shape in (
                (8, 2, 4, per_y, HALF),
                (8, 2, 4, per_y, HALF),
                (8, 2, 4, per_y, HALF),
                (14, 4, na, HALF),
                (4, 6, 2, 2, nb, 128),
                (4, 6, 2, nc, HALF),
                (8, 4, nb, 128),
                (8, 2, nc, HALF),
                (2, 4, na, HALF),
                (4, 3, 2, nb, 128),
                (4, 3, 2, nc, 128),
                (8, nb + nc, 128),
                (7, nb + nc, 128),
                (15, na, 128),
                (per_y, 128),
            )
        ]
    out = pl.pallas_call(
        kernel,
        out_shape=pltpu.VMEM((ROWS, C), F32),
        in_specs=[
            pl.BlockSpec(memory_space=pl.ANY),
            pl.BlockSpec(memory_space=pltpu.VMEM),
            pl.BlockSpec(memory_space=pl.ANY),
        ],
        out_specs=pl.BlockSpec(memory_space=pltpu.VMEM),
        scratch_shapes=scratch,
        compiler_params=pltpu.CompilerParams(
            collective_id=0, has_side_effects=True, vmem_limit_bytes=58 << 20
        ),
    )(hidden, gain.reshape(1, D), d_query)
    return out


def solution(mesh):
    both = ("row", "col")
    return jax.shard_map(
        per_device,
        mesh=mesh,
        in_specs=(P(both, None), P(), P(both, None)),
        out_specs=P("row", None),
        check_vma=False,
    )
```

```python
import jax
import jax.numpy as jnp
from jax import lax
from jax.experimental import pallas as pl
from jax.experimental.pallas import tpu as pltpu
from jax.sharding import PartitionSpec as P

D = 6144
C = 512
T = 768
ROWS = 384
HALF = C // 2
CHUNKS = ((3, 4, 4, 4),)
ORDER = (4, 3, -3, 2, -2, 1, -1, 0)
WORK, FIN, A_STEP, RING_FIRST, RING_SECOND, RING_END, STAGE3, A_END, BC_END, A_GATHER, FORWARD, FINISH, A_MID = range(13)
EVENTS = (
    (WORK, 0, 0), (WORK, 0, 1), (WORK, 0, 2), (WORK, 0, 3), (FIN, 0, 0), (A_STEP, 0, 0),
    (WORK, 0, 4), (FIN, 0, 1), (RING_FIRST, 0, 0), (WORK, 0, 5), (FIN, 0, 2), (A_STEP, 0, 1),
    (FIN, 0, 3), (RING_FIRST, 0, 1), (WORK, 0, 6), (WORK, 0, 7), (A_STEP, 0, 2), (FIN, 0, 4),
    (FIN, 0, 5), (RING_SECOND, 0, 0), (RING_FIRST, 0, 2), (FIN, 0, 6), (A_STEP, 0, 3), (FIN, 0, 7),
    (RING_FIRST, 0, 3), (A_STEP, 0, 4), (RING_SECOND, 0, 1), (A_STEP, 0, 5), (RING_END, 0, 0), (RING_SECOND, 0, 2),
    (RING_SECOND, 0, 3), (A_STEP, 0, 6), (RING_END, 0, 1), (STAGE3, 0, 0), (RING_END, 0, 2), (RING_END, 0, 3),
    (STAGE3, 0, 1), (A_END, 0, 0), (STAGE3, 0, 2), (STAGE3, 0, 3), (A_MID, 0, 0), (BC_END, 0, 0),
    (A_GATHER, 0, 0), (FORWARD, 0, 0), (FINISH, 0, 0),
)
SUB = 32
WSUB = 64
F32 = jnp.float32
MESH = pl.DeviceIdType.MESH
N_SEM = 144 * len(CHUNKS)


def kernel(h_hbm, gain, dq_hbm, O, h, dq, nb, mean_s, rstd_s, in_sem, ss, rs, *buffers):
    r, c = lax.axis_index("row"), lax.axis_index("col")
    z, xlo = r // 2, lax.rem(r, 2)
    xhi, y, core = c // 8, lax.rem(c // 2, 4), lax.rem(c, 2)
    x = xhi * 2 + xlo

    def device(dx=0, dy=0, dz=0, flip=0):
        nx, ny = lax.rem(x + dx + 4, 4), lax.rem(y + dy + 4, 4)
        nz, ncore = lax.rem(z + dz + 8, 8), lax.rem(core + flip, 2)
        return (nz * 2 + lax.rem(nx, 2), (nx // 2) * 8 + ny * 2 + ncore)

    def lanes(block, width=128):
        return pl.ds(pl.multiple_of(block * width, width), width)

    count = [0]
    sent = []

    def send(src, dst, **where):
        k = count[0]
        count[0] += 1
        copy = pltpu.make_async_remote_copy(
            src, dst, ss.at[k], rs.at[k], device_id=device(**where), device_id_type=MESH
        )
        copy.start()
        sent.append(copy)
        return copy

    loads = [
        pltpu.make_async_copy(h_hbm.at[pl.ds(k * 128, 128)], h.at[pl.ds(k * 128, 128)], in_sem.at[k])
        for k in range(T // 128)
    ]
    for copy in loads:
        copy.start()
    load_own = pltpu.make_async_copy(dq_hbm.at[:, lanes(core, HALF)], dq.at[:, 0:HALF], in_sem.at[6])
    load_peer = pltpu.make_async_copy(dq_hbm.at[:, lanes(1 - core, HALF)], dq.at[:, HALF:C], in_sem.at[7])
    load_own.start()
    load_peer.start()

    plane = [(dx, dy) for dx in range(4) for dy in range(4) if (dx, dy) != (0, 0)]
    barrier = pltpu.get_barrier_semaphore()
    partners = [dict(flip=1)] + [dict(dz=k) for k in range(1, 8)] + [dict(dx=dx, dy=dy) for dx, dy in plane if dx in (0, 2) or dy == 0]
    for where in partners:
        pl.semaphore_signal(barrier, inc=1, device_id=device(**where), device_id_type=MESH)

    for k, copy in enumerate(loads):
        copy.wait()

        @pl.loop(0, 128 // SUB, unroll=True)
        def _(b):
            rows = pl.ds(pl.multiple_of(k * 128 + b * SUB, SUB), SUB)
            first = h[rows, 0:128].astype(F32)
            shift = jnp.broadcast_to(jnp.sum(first, axis=1, keepdims=True) * (1.0 / 128), (SUB, 128))
            total = jnp.zeros((SUB, 128), F32)
            square = jnp.zeros((SUB, 128), F32)
            for t in range(D // 128):
                apart = h[rows, t * 128 : (t + 1) * 128].astype(F32) - shift
                total += apart
                square += apart * apart
            off = jnp.sum(total, axis=1, keepdims=True) * (1.0 / D)
            var = jnp.maximum(jnp.sum(square, axis=1, keepdims=True) * (1.0 / D) - off * off, 0.0)
            mean_s[rows, :] = shift + jnp.broadcast_to(off, (SUB, 128))
            rstd_s[rows, :] = jnp.broadcast_to(lax.rsqrt(var + 1e-06), (SUB, 128))

    load_own.wait()
    load_peer.wait()
    pl.semaphore_wait(barrier, len(partners))

    def target_x(dx):
        nx = lax.rem(x + dx + 4, 4)
        return lax.rem(nx, 2), nx // 2

    def target_y(dy):
        return lax.rem(y + dy + 4, 4)

    mine = lanes(core * 2 + xhi)
    half_mine = lanes(core, HALF)
    owners = [(dx, dy) for dx, dy in plane if dx in (0, 2)]

    def chunk(q):
        w, na, nb_, nc = (v * m for v, m in zip(CHUNKS[q], (1, 8, 8, 8)))
        tile0 = sum(CHUNKS[k][0] for k in range(q))
        b0, c0 = na, na + nb_
        per_y = 32 * w
        S, X, RP, RA, RB, RC, TB, TC, TA, RB2, RC2, U, RZ, RA1, TM, RA2, PF = buffers[q * 17 : q * 17 + 17]
        pairs, ring, second, third, a_sent, a_plane, gathered, last = {}, {}, {}, {}, {}, [], [], []

        def normalise(i, slot):
            group = lax.rem(z + ORDER[i] + 8, 8) * 2
            for b in range(T // WSUB):
                rows = pl.ds(b * WSUB, WSUB)
                mean, rstd = mean_s[rows, :], rstd_s[rows, :]
                for t in range(2 * w):
                    cols = lanes((group + t // w) * 3 + tile0 + t % w)
                    centred = h[rows, cols].astype(F32) - mean
                    nb[slot, rows, t * 128 : (t + 1) * 128] = (centred * rstd * gain[:, cols]).astype(jnp.bfloat16)

        def work(i):
            slot = i % 2

            for g in range(2):
                product = lax.dot_general(
                    nb[slot, :, g * 128 * w : (g + 1) * 128 * w], dq[...], (((0,), (0,)), ((), ())),
                    preferred_element_type=F32,
                )
                X[i, g] = product[:, HALF:].reshape(4, per_y, HALF)
                S[i, g] = product[:, :HALF].reshape(4, per_y, HALF)
            pairs[i] = send(X.at[i], RP.at[i], flip=1)
            if i < 7:
                normalise(i + 1, 1 - slot)
            elif q + 1 < len(CHUNKS):
                chunks[q + 1][-1](0, 1 - slot)

        def fin(i):
            pairs[i].wait_recv()
            S[i] += RP[i]

        def b_block(i, dx, half):
            low, high = target_x(dx)
            return (pl.ds(i, 2), low, pl.ds(half * 2, 2), pl.ds(b0, nb_), lanes(high))

        def c_block(i, dy, half):
            return (pl.ds(i, 2), half, target_y(dy), pl.ds(c0, nc))

        def a_block(i, g):
            return (i, g, slice(None), pl.ds(0, na))

        both = ((RB, b_block, "dx"), (RC, c_block, "dy"))

        def ring_first(j):
            i = 2 * j
            for s, (R, block, axis) in enumerate(both):
                ring[s, j] = [
                    send(S.at[block(i, 2, 0)], R.at[j, 0], **{axis: 1}),
                    send(S.at[block(i, 2, 1)], R.at[j, 1], **{axis: -1}),
                    send(S.at[block(i, 1, 1)], R.at[j, 2], **{axis: 1}),
                    send(S.at[block(i, -1, 0)], R.at[j, 3], **{axis: -1}),
                ]

        def ring_second(j):
            i = 2 * j
            for s, (R, block, axis) in enumerate(both):
                for slot, d, half in ((0, 1, 0), (1, -1, 1)):
                    ring[s, j][slot].wait_recv()
                    R[j, slot] += S[block(i, d, half)]
                    ring[s, j].append(send(R.at[j, slot], R.at[j, 4 + slot], **{axis: d}))

        def ring_end(j):
            i = 2 * j
            for s in range(2):
                for slot in range(2, 6):
                    ring[s, j][slot].wait_recv()
            for half, (p, r) in enumerate(((3, 4), (2, 5))):
                TB[pl.ds(i, 2), pl.ds(half * 2, 2)] = S[b_block(i, 0, half)] + RB[j, p] + RB[j, r]
                TC[pl.ds(i, 2), half] = S[c_block(i, 0, half)] + RC[j, p] + RC[j, r]
            for k in range(1, 4):
                low, high = target_x(k)
                second[0, j, k] = send(TB.at[pl.ds(i, 2), target_y(k)], RB2.at[j, k - 1], dy=k)
                second[1, j, k] = send(TC.at[pl.ds(i, 2), low, :, lanes(high)], RC2.at[j, k - 1], dx=k)

        def stage3(j):
            i = 2 * j
            for k in range(1, 4):
                second[0, j, k].wait_recv()
                second[1, j, k].wait_recv()
            part_b = TB[pl.ds(i, 2), y]
            part_c = TC[pl.ds(i, 2), xlo, :, lanes(xhi)]
            for k in range(3):
                part_b += RB2[j, k]
                part_c += RC2[j, k]
            U[pl.ds(i, 2), 0:nb_] = part_b
            U[pl.ds(i, 2), nb_ : nb_ + nc] = part_c
            for k in range(i, min(i + 2, 7)):
                third[k] = send(U.at[k], RZ.at[k], dz=ORDER[k])

        up = ((0, 0, 0, None), (1, 1, 1, None), (2, 1, 0, 0), (3, 3, 1, 1), (4, 3, 0, 2), (5, 5, 1, 3), (6, 5, 0, 4))
        down = ((7, 0, 1, None), (8, 2, 0, None), (9, 2, 1, 7), (10, 4, 0, 8), (11, 4, 1, 9), (12, 6, 0, 10), (13, 6, 1, 11))

        def a_step(k):
            for (slot, i, g, add), dz in ((up[k], 1), (down[k], -1)):
                if add is None:
                    a_sent[slot] = send(S.at[a_block(i, g)], RA.at[slot], dz=dz)
                else:
                    a_sent[add].wait_recv()
                    RA[add] += S[a_block(i, g)]
                    a_sent[slot] = send(RA.at[add], RA.at[slot], dz=dz)

        def a_end(_):
            for g, (p, r) in enumerate(((6, 12), (5, 13))):
                a_sent[p].wait_recv()
                a_sent[r].wait_recv()
                TA[g] = S[a_block(7, g)] + RA[p] + RA[r]
            for k in range(1, 4):
                low, high = target_x(k)
                a_plane.append(send(TA.at[low, :, :, lanes(high)], RA1.at[k - 1], dx=k))

        def a_mid(_):
            total = TA[xlo, :, :, lanes(xhi)]
            for k in range(3):
                a_plane[k].wait_recv()
                total += RA1[k]
            TM[...] = total
            for k in range(1, 4):
                a_plane.append(send(TM.at[target_y(k)], RA2.at[k - 1], dy=k))

        def gather(first, n):
            rows = pl.ds(pl.multiple_of(tile0 * 128 + y * per_y + first, 8), n)
            O[rows, mine] = PF[pl.ds(first, n)]
            here = O.at[rows, mine]
            gathered.append((None, here))
            for dx, dy in owners:
                ny, nhigh = target_y(-dy), target_x(-dx)[1]
                there = O.at[pl.ds(pl.multiple_of(tile0 * 128 + ny * per_y + first, 8), n), lanes(core * 2 + nhigh)]
                gathered.append((send(PF.at[pl.ds(first, n)], here, dx=dx, dy=dy), there))

        def bc_end(_):
            for k in range(7):
                third[k].wait_recv()
            total = U[7]
            for k in range(7):
                total += RZ[k]
            PF[b0:per_y] = total
            gather(b0, nb_ + nc)

        def a_gather(_):
            total = TM[y]
            for k in range(3):
                a_plane[3 + k].wait_recv()
                total += RA2[k]
            PF[0:na] = total
            gather(0, na)

        def forward(_):
            for copy, part in gathered:
                if copy is not None:
                    copy.wait_recv()
                last.append(send(part, part, flip=1))

        def finish(_):
            for copy in last:
                copy.wait_recv()

        return (work, fin, a_step, ring_first, ring_second, ring_end, stage3, a_end, bc_end, a_gather, forward, finish, a_mid, normalise)

    chunks = [chunk(q) for q in range(len(CHUNKS))]
    chunks[0][-1](0, 0)
    for event, q, k in EVENTS:
        chunks[q][event](k)
    for copy in sent:
        copy.wait_send()


def per_device(hidden, gain, d_query):
    scratch = [
        pltpu.VMEM((T, D), jnp.bfloat16),
        pltpu.VMEM((T, C), jnp.bfloat16),
        pltpu.VMEM((2, T, 256 * max(w for w, *_ in CHUNKS)), jnp.bfloat16),
        pltpu.VMEM((T, 128), F32),
        pltpu.VMEM((T, 128), F32),
        pltpu.SemaphoreType.DMA((8,)),
        pltpu.SemaphoreType.DMA((N_SEM,)),
        pltpu.SemaphoreType.DMA((N_SEM,)),
    ]
    for w, a, b, c in CHUNKS:
        na, nb, nc, per_y = 8 * a, 8 * b, 8 * c, 32 * w
        scratch += [
            pltpu.VMEM(shape, F32)
            for shape in (
                (8, 2, 4, per_y, HALF),
                (8, 2, 4, per_y, HALF),
                (8, 2, 4, per_y, HALF),
                (14, 4, na, HALF),
                (4, 6, 2, 2, nb, 128),
                (4, 6, 2, nc, HALF),
                (8, 4, nb, 128),
                (8, 2, nc, HALF),
                (2, 4, na, HALF),
                (4, 3, 2, nb, 128),
                (4, 3, 2, nc, 128),
                (8, nb + nc, 128),
                (7, nb + nc, 128),
                (3, 4, na, 128),
                (4, na, 128),
                (3, na, 128),
                (per_y, 128),
            )
        ]
    out = pl.pallas_call(
        kernel,
        out_shape=pltpu.VMEM((ROWS, C), F32),
        in_specs=[
            pl.BlockSpec(memory_space=pl.ANY),
            pl.BlockSpec(memory_space=pltpu.VMEM),
            pl.BlockSpec(memory_space=pl.ANY),
        ],
        out_specs=pl.BlockSpec(memory_space=pltpu.VMEM),
        scratch_shapes=scratch,
        compiler_params=pltpu.CompilerParams(
            collective_id=0, has_side_effects=True, vmem_limit_bytes=58 << 20
        ),
    )(hidden, gain.reshape(1, D), d_query)
    return out


def solution(mesh):
    both = ("row", "col")
    return jax.shard_map(
        per_device,
        mesh=mesh,
        in_specs=(P(both, None), P(), P(both, None)),
        out_specs=P("row", None),
        check_vma=False,
    )
```

```python
import jax
import jax.numpy as jnp
from jax import lax
from jax.experimental import pallas as pl
from jax.experimental.pallas import tpu as pltpu
from jax.sharding import PartitionSpec as P

D = 6144
C = 512
T = 768
ROWS = 384
HALF = C // 2
CHUNKS = ((3, 4, 4, 4),)
ORDER = (4, 3, -3, 2, -2, 1, -1, 0)
WORK, FIN, A_STEP, RING_FIRST, RING_SECOND, RING_END, STAGE3, A_END, BC_END, A_GATHER, FORWARD, FINISH, A_MID = range(13)
EVENTS = (
    (WORK, 0, 0), (WORK, 0, 1), (WORK, 0, 2), (FIN, 0, 0), (A_STEP, 0, 0), (WORK, 0, 3),
    (FIN, 0, 1), (RING_FIRST, 0, 0), (WORK, 0, 4), (FIN, 0, 2), (A_STEP, 0, 1), (WORK, 0, 5),
    (FIN, 0, 3), (RING_FIRST, 0, 1), (A_STEP, 0, 2), (WORK, 0, 6), (FIN, 0, 4), (RING_SECOND, 0, 0),
    (WORK, 0, 7), (FIN, 0, 5), (RING_FIRST, 0, 2), (A_STEP, 0, 3), (FIN, 0, 6), (FIN, 0, 7),
    (RING_FIRST, 0, 3), (RING_SECOND, 0, 1), (A_STEP, 0, 4), (RING_END, 0, 0), (RING_SECOND, 0, 2), (A_STEP, 0, 5),
    (A_STEP, 0, 6), (RING_END, 0, 1), (RING_SECOND, 0, 3), (STAGE3, 0, 0), (RING_END, 0, 2), (STAGE3, 0, 1),
    (RING_END, 0, 3), (STAGE3, 0, 2), (A_END, 0, 0), (STAGE3, 0, 3), (A_MID, 0, 0), (BC_END, 0, 0),
    (A_GATHER, 0, 0), (FORWARD, 0, 0), (FINISH, 0, 0),
)
SUB = 32
WSUB = 64
F32 = jnp.float32
MESH = pl.DeviceIdType.MESH
N_SEM = 144 * len(CHUNKS)


def kernel(h_hbm, gain, dq_hbm, O, h, dq, nb, mean_s, rstd_s, in_sem, ss, rs, *buffers):
    r, c = lax.axis_index("row"), lax.axis_index("col")
    z, xlo = r // 2, lax.rem(r, 2)
    xhi, y, core = c // 8, lax.rem(c // 2, 4), lax.rem(c, 2)
    x = xhi * 2 + xlo

    def device(dx=0, dy=0, dz=0, flip=0):
        nx, ny = lax.rem(x + dx + 4, 4), lax.rem(y + dy + 4, 4)
        nz, ncore = lax.rem(z + dz + 8, 8), lax.rem(core + flip, 2)
        return (nz * 2 + lax.rem(nx, 2), (nx // 2) * 8 + ny * 2 + ncore)

    def lanes(block, width=128):
        return pl.ds(pl.multiple_of(block * width, width), width)

    count = [0]
    sent = []

    def send(src, dst, **where):
        k = count[0]
        count[0] += 1
        copy = pltpu.make_async_remote_copy(
            src, dst, ss.at[k], rs.at[k], device_id=device(**where), device_id_type=MESH
        )
        copy.start()
        sent.append(copy)
        return copy

    loads = [
        pltpu.make_async_copy(h_hbm.at[pl.ds(k * 128, 128)], h.at[pl.ds(k * 128, 128)], in_sem.at[k])
        for k in range(T // 128)
    ]
    for copy in loads:
        copy.start()
    load_own = pltpu.make_async_copy(dq_hbm.at[:, lanes(core, HALF)], dq.at[:, 0:HALF], in_sem.at[6])
    load_peer = pltpu.make_async_copy(dq_hbm.at[:, lanes(1 - core, HALF)], dq.at[:, HALF:C], in_sem.at[7])
    load_own.start()
    load_peer.start()

    plane = [(dx, dy) for dx in range(4) for dy in range(4) if (dx, dy) != (0, 0)]
    barrier = pltpu.get_barrier_semaphore()
    partners = [dict(flip=1)] + [dict(dz=k) for k in range(1, 8)] + [dict(dx=dx, dy=dy) for dx, dy in plane if dx in (0, 2) or dy == 0]
    for where in partners:
        pl.semaphore_signal(barrier, inc=1, device_id=device(**where), device_id_type=MESH)

    for k, copy in enumerate(loads):
        copy.wait()

        @pl.loop(0, 128 // SUB, unroll=True)
        def _(b):
            rows = pl.ds(pl.multiple_of(k * 128 + b * SUB, SUB), SUB)
            first = h[rows, 0:128].astype(F32)
            shift = jnp.broadcast_to(jnp.sum(first, axis=1, keepdims=True) * (1.0 / 128), (SUB, 128))
            total = jnp.zeros((SUB, 128), F32)
            square = jnp.zeros((SUB, 128), F32)
            for t in range(D // 128):
                apart = h[rows, t * 128 : (t + 1) * 128].astype(F32) - shift
                total += apart
                square += apart * apart
            off = jnp.sum(total, axis=1, keepdims=True) * (1.0 / D)
            var = jnp.maximum(jnp.sum(square, axis=1, keepdims=True) * (1.0 / D) - off * off, 0.0)
            mean_s[rows, :] = shift + jnp.broadcast_to(off, (SUB, 128))
            rstd_s[rows, :] = jnp.broadcast_to(lax.rsqrt(var + 1e-06), (SUB, 128))

    load_own.wait()
    load_peer.wait()
    pl.semaphore_wait(barrier, len(partners))

    def target_x(dx):
        nx = lax.rem(x + dx + 4, 4)
        return lax.rem(nx, 2), nx // 2

    def target_y(dy):
        return lax.rem(y + dy + 4, 4)

    mine = lanes(core * 2 + xhi)
    half_mine = lanes(core, HALF)
    owners = [(dx, dy) for dx, dy in plane if dx in (0, 2)]

    def chunk(q):
        w, na, nb_, nc = (v * m for v, m in zip(CHUNKS[q], (1, 8, 8, 8)))
        tile0 = sum(CHUNKS[k][0] for k in range(q))
        b0, c0 = na, na + nb_
        per_y = 32 * w
        S, X, RP, RA, RB, RC, TB, TC, TA, RB2, RC2, U, RZ, RA1, TM, RA2, PF = buffers[q * 17 : q * 17 + 17]
        pairs, ring, second, third, a_sent, a_plane, gathered, last = {}, {}, {}, {}, {}, [], [], []

        def normalise(i, slot):
            group = lax.rem(z + ORDER[i] + 8, 8) * 2
            for b in range(T // WSUB):
                rows = pl.ds(b * WSUB, WSUB)
                mean, rstd = mean_s[rows, :], rstd_s[rows, :]
                for t in range(2 * w):
                    cols = lanes((group + t // w) * 3 + tile0 + t % w)
                    centred = h[rows, cols].astype(F32) - mean
                    nb[slot, rows, t * 128 : (t + 1) * 128] = (centred * rstd * gain[:, cols]).astype(jnp.bfloat16)

        def work(i):
            slot = i % 2

            for g in range(2):
                product = lax.dot_general(
                    nb[slot, :, g * 128 * w : (g + 1) * 128 * w], dq[...], (((0,), (0,)), ((), ())),
                    preferred_element_type=F32,
                )
                X[i, g] = product[:, HALF:].reshape(4, per_y, HALF)
                S[i, g] = product[:, :HALF].reshape(4, per_y, HALF)
            pairs[i] = send(X.at[i], RP.at[i], flip=1)
            if i < 7:
                normalise(i + 1, 1 - slot)
            elif q + 1 < len(CHUNKS):
                chunks[q + 1][-1](0, 1 - slot)

        def fin(i):
            pairs[i].wait_recv()
            S[i] += RP[i]

        def b_block(i, dx, half):
            low, high = target_x(dx)
            return (pl.ds(i, 2), low, pl.ds(half * 2, 2), pl.ds(b0, nb_), lanes(high))

        def c_block(i, dy, half):
            return (pl.ds(i, 2), half, target_y(dy), pl.ds(c0, nc))

        def a_block(i, g):
            return (i, g, slice(None), pl.ds(0, na))

        both = ((RB, b_block, "dx"), (RC, c_block, "dy"))

        def ring_first(j):
            i = 2 * j
            for s, (R, block, axis) in enumerate(both):
                ring[s, j] = [
                    send(S.at[block(i, 2, 0)], R.at[j, 0], **{axis: 1}),
                    send(S.at[block(i, 2, 1)], R.at[j, 1], **{axis: -1}),
                    send(S.at[block(i, 1, 1)], R.at[j, 2], **{axis: 1}),
                    send(S.at[block(i, -1, 0)], R.at[j, 3], **{axis: -1}),
                ]

        def ring_second(j):
            i = 2 * j
            for s, (R, block, axis) in enumerate(both):
                for slot, d, half in ((0, 1, 0), (1, -1, 1)):
                    ring[s, j][slot].wait_recv()
                    R[j, slot] += S[block(i, d, half)]
                    ring[s, j].append(send(R.at[j, slot], R.at[j, 4 + slot], **{axis: d}))

        def ring_end(j):
            i = 2 * j
            for s in range(2):
                for slot in range(2, 6):
                    ring[s, j][slot].wait_recv()
            for half, (p, r) in enumerate(((3, 4), (2, 5))):
                TB[pl.ds(i, 2), pl.ds(half * 2, 2)] = S[b_block(i, 0, half)] + RB[j, p] + RB[j, r]
                TC[pl.ds(i, 2), half] = S[c_block(i, 0, half)] + RC[j, p] + RC[j, r]
            for k in range(1, 4):
                low, high = target_x(k)
                second[0, j, k] = send(TB.at[pl.ds(i, 2), target_y(k)], RB2.at[j, k - 1], dy=k)
                second[1, j, k] = send(TC.at[pl.ds(i, 2), low, :, lanes(high)], RC2.at[j, k - 1], dx=k)

        def stage3(j):
            i = 2 * j
            for k in range(1, 4):
                second[0, j, k].wait_recv()
                second[1, j, k].wait_recv()
            part_b = TB[pl.ds(i, 2), y]
            part_c = TC[pl.ds(i, 2), xlo, :, lanes(xhi)]
            for k in range(3):
                part_b += RB2[j, k]
                part_c += RC2[j, k]
            U[pl.ds(i, 2), 0:nb_] = part_b
            U[pl.ds(i, 2), nb_ : nb_ + nc] = part_c
            for k in range(i, min(i + 2, 7)):
                third[k] = send(U.at[k], RZ.at[k], dz=ORDER[k])

        up = ((0, 0, 0, None), (1, 1, 1, None), (2, 1, 0, 0), (3, 3, 1, 1), (4, 3, 0, 2), (5, 5, 1, 3), (6, 5, 0, 4))
        down = ((7, 0, 1, None), (8, 2, 0, None), (9, 2, 1, 7), (10, 4, 0, 8), (11, 4, 1, 9), (12, 6, 0, 10), (13, 6, 1, 11))

        def a_step(k):
            for (slot, i, g, add), dz in ((up[k], 1), (down[k], -1)):
                if add is None:
                    a_sent[slot] = send(S.at[a_block(i, g)], RA.at[slot], dz=dz)
                else:
                    a_sent[add].wait_recv()
                    RA[add] += S[a_block(i, g)]
                    a_sent[slot] = send(RA.at[add], RA.at[slot], dz=dz)

        def a_end(_):
            for g, (p, r) in enumerate(((6, 12), (5, 13))):
                a_sent[p].wait_recv()
                a_sent[r].wait_recv()
                TA[g] = S[a_block(7, g)] + RA[p] + RA[r]
            for k in range(1, 4):
                low, high = target_x(k)
                a_plane.append(send(TA.at[low, :, :, lanes(high)], RA1.at[k - 1], dx=k))

        def a_mid(_):
            total = TA[xlo, :, :, lanes(xhi)]
            for k in range(3):
                a_plane[k].wait_recv()
                total += RA1[k]
            TM[...] = total
            for k in range(1, 4):
                a_plane.append(send(TM.at[target_y(k)], RA2.at[k - 1], dy=k))

        def gather(first, n):
            rows = pl.ds(pl.multiple_of(tile0 * 128 + y * per_y + first, 8), n)
            O[rows, mine] = PF[pl.ds(first, n)]
            here = O.at[rows, mine]
            gathered.append((None, here))
            for dx, dy in owners:
                ny, nhigh = target_y(-dy), target_x(-dx)[1]
                there = O.at[pl.ds(pl.multiple_of(tile0 * 128 + ny * per_y + first, 8), n), lanes(core * 2 + nhigh)]
                gathered.append((send(PF.at[pl.ds(first, n)], here, dx=dx, dy=dy), there))

        def bc_end(_):
            for k in range(7):
                third[k].wait_recv()
            total = U[7]
            for k in range(7):
                total += RZ[k]
            PF[b0:per_y] = total
            gather(b0, nb_ + nc)

        def a_gather(_):
            total = TM[y]
            for k in range(3):
                a_plane[3 + k].wait_recv()
                total += RA2[k]
            PF[0:na] = total
            gather(0, na)

        def forward(_):
            for copy, part in gathered:
                if copy is not None:
                    copy.wait_recv()
                last.append(send(part, part, flip=1))

        def finish(_):
            for copy in last:
                copy.wait_recv()

        return (work, fin, a_step, ring_first, ring_second, ring_end, stage3, a_end, bc_end, a_gather, forward, finish, a_mid, normalise)

    chunks = [chunk(q) for q in range(len(CHUNKS))]
    chunks[0][-1](0, 0)
    for event, q, k in EVENTS:
        chunks[q][event](k)
    for copy in sent:
        copy.wait_send()


def per_device(hidden, gain, d_query):
    scratch = [
        pltpu.VMEM((T, D), jnp.bfloat16),
        pltpu.VMEM((T, C), jnp.bfloat16),
        pltpu.VMEM((2, T, 256 * max(w for w, *_ in CHUNKS)), jnp.bfloat16),
        pltpu.VMEM((T, 128), F32),
        pltpu.VMEM((T, 128), F32),
        pltpu.SemaphoreType.DMA((8,)),
        pltpu.SemaphoreType.DMA((N_SEM,)),
        pltpu.SemaphoreType.DMA((N_SEM,)),
    ]
    for w, a, b, c in CHUNKS:
        na, nb, nc, per_y = 8 * a, 8 * b, 8 * c, 32 * w
        scratch += [
            pltpu.VMEM(shape, F32)
            for shape in (
                (8, 2, 4, per_y, HALF),
                (8, 2, 4, per_y, HALF),
                (8, 2, 4, per_y, HALF),
                (14, 4, na, HALF),
                (4, 6, 2, 2, nb, 128),
                (4, 6, 2, nc, HALF),
                (8, 4, nb, 128),
                (8, 2, nc, HALF),
                (2, 4, na, HALF),
                (4, 3, 2, nb, 128),
                (4, 3, 2, nc, 128),
                (8, nb + nc, 128),
                (7, nb + nc, 128),
                (3, 4, na, 128),
                (4, na, 128),
                (3, na, 128),
                (per_y, 128),
            )
        ]
    out = pl.pallas_call(
        kernel,
        out_shape=pltpu.VMEM((ROWS, C), F32),
        in_specs=[
            pl.BlockSpec(memory_space=pl.ANY),
            pl.BlockSpec(memory_space=pltpu.VMEM),
            pl.BlockSpec(memory_space=pl.ANY),
        ],
        out_specs=pl.BlockSpec(memory_space=pltpu.VMEM),
        scratch_shapes=scratch,
        compiler_params=pltpu.CompilerParams(
            collective_id=0, has_side_effects=True, vmem_limit_bytes=58 << 20
        ),
    )(hidden, gain.reshape(1, D), d_query)
    return out


def solution(mesh):
    both = ("row", "col")
    return jax.shard_map(
        per_device,
        mesh=mesh,
        in_specs=(P(both, None), P(), P(both, None)),
        out_specs=P("row", None),
        check_vma=False,
    )
```
